256 devices in a mesh: dp: 4 (over z_hi), mx: 8 (over z_lo, y), my: 8 (over x, core).
Axes of the slice: x: 4, y: 4, z: 8 (z_hi: 4, z_lo: 2; z = z_hi * 2 + z_lo), core: 2. Of those that a mesh axis runs over, the one named last changes fastest.
Arguments:
- inputs: bfloat16 [768, 4096], P(('dp', 'mx', 'my')), may hold values from -6 to 6
- weight_means: bfloat16 [3, 14336, 4096], P(None, ('mx', 'my'), 'dp'), may hold values from -6 to 6
- weight_sigmas: bfloat16 [3, 14336, 4096], P(None, ('mx', 'my'), 'dp'), may hold values from 0.099609375 to 1
- weight_noise: bfloat16 [3, 14336, 4096], P(None, ('mx', 'my'), 'dp'), may hold values from -6 to 6
- input_signs: int32 [768, 4096], P(('dp', 'mx', 'my')), may hold values 0 or 1
- output_signs: int32 [2, 14336, 768], P(None, ('mx', 'my'), 'dp'), may hold values 0 or 1
- hidden_signs: int32 [14336, 768], P(('mx', 'my'), 'dp'), may hold values 0 or 1
- result_signs: int32 [768, 4096], P(('dp', 'mx', 'my')), may hold values 0 or 1
- cotangent: bfloat16 [768, 4096], P(('dp', 'mx', 'my')), may hold values from -6 to 6
Outputs:
- result: bfloat16 [768, 4096], P(('dp', 'mx', 'my'))
- input_grad: bfloat16 [768, 4096], P(('dp', 'mx', 'my'))
- mean_grad: bfloat16 [3, 14336, 4096], P(None, ('mx', 'my'), 'dp')
- sigma_grad: bfloat16 [3, 14336, 4096], P(None, ('mx', 'my'), 'dp')
The draws below stay inside these ranges and needn't reach their ends.
All inputs are finite; a program needn't handle non-finite values. No bound on the sum of `input_signs` or of `output_signs` or of `hidden_signs` or of `result_signs` on one device may be relied on, other than what follows from the above.
Results may differ from the reference program's by a relative error of at most 0.02.
Values may be sent and summed in bfloat16 or wider, within the bound.
No kernel may reach another device: no remote copies, remote signals or barrier semaphores. Data moves between devices by JAX's collectives and lax.ppermute only.
A program may use at most 128 MiB of HBM per device.

```python
import math
import jax
import jax.numpy as jnp
from jax import lax

D = 4096
FF = 14336
TOK_DEV = 192
TOKENS = 768
N_DP = 4


def with_ends(array, own_key, least, largest):
    longest = array.shape.index(max(array.shape))
    spots = []
    for shift in (0, 1):
        where = [jax.random.randint(jax.random.fold_in(own_key, axis), (), 0, length) for axis, length in enumerate(array.shape)]
        where[longest] = (where[longest] + shift) % array.shape[longest]
        spots.append(tuple(where))
    return array.at[spots[0]].set(least).at[spots[1]].set(largest)


def levels(stream_key, dims, shards, low, top_value):
    def one(axis_at, shards_of):
        heights = jax.random.uniform(jax.random.fold_in(jax.random.fold_in(stream_key, 6), axis_at), (shards_of,), jnp.float32, low / len(shards), top_value / len(shards))
        return jnp.repeat(jnp.exp(heights), dims[axis_at] // shards_of).reshape((-1,) + (1,) * (len(dims) - axis_at - 1))

    level = one(*shards[0])
    for cut in shards[1:]:
        level = level * one(*cut)
    return level


def gaussian(own_key, shape, scale, bound, split=(), dtype=jnp.bfloat16):
    loudness = levels(own_key, shape, split, -0.22, 0.18) if split else 1.0
    drawn = jax.random.normal(own_key, shape, jnp.float32) * scale * loudness
    return jnp.minimum(jnp.maximum(drawn, -bound), bound).astype(dtype)


def setup_inputs(seed: int = 0) -> dict:
    key_of = jax.random.split(jax.random.key(seed), 10)
    inputs = gaussian(key_of[0], (TOKENS, D), 1.0, 6.0, ((0, 256),))
    weight_means = gaussian(key_of[1], (3, FF, D), 1.0, 6.0, ((1, 64), (2, 4)))
    weight_sigmas = jnp.clip(jnp.exp(math.log(1.0) - 2.306499 * jax.random.uniform(key_of[2], (3, FF, D), jnp.float32) ** levels(key_of[2], (3, FF, D), ((1, 64), (2, 4)), -0.2, 0.2)), 0.099609375, 1.0).astype(jnp.bfloat16)
    weight_noise = gaussian(key_of[3], (3, FF, D), 1.0, 6.0, ((1, 64), (2, 4)))
    input_signs = with_ends((jax.random.randint(key_of[4], (TOKENS, D), 0, 2) < 1).astype(jnp.int32), jax.random.fold_in(key_of[4], 1), 0, 1)
    output_signs = with_ends((jax.random.randint(key_of[5], (2, FF, TOKENS), 0, 2) < 1).astype(jnp.int32), jax.random.fold_in(key_of[5], 1), 0, 1)
    hidden_signs = with_ends((jax.random.randint(key_of[6], (FF, TOKENS), 0, 2) < 1).astype(jnp.int32), jax.random.fold_in(key_of[6], 1), 0, 1)
    result_signs = with_ends((jax.random.randint(key_of[7], (TOKENS, D), 0, 2) < 1).astype(jnp.int32), jax.random.fold_in(key_of[7], 1), 0, 1)
    cotangent = gaussian(key_of[8], (TOKENS, D), 1.0, 6.0, ((0, 256),))
    return {"inputs": inputs, "weight_means": weight_means, "weight_sigmas": weight_sigmas, "weight_noise": weight_noise, "input_signs": input_signs, "output_signs": output_signs, "hidden_signs": hidden_signs, "result_signs": result_signs, "cotangent": cotangent}


def to_sign(values):
    return (2 * values - 1).astype(jnp.float32)


def reference(inputs, weight_means, weight_sigmas, weight_noise, input_signs, output_signs, hidden_signs, result_signs, cotangent):
    scale_in = D ** -0.5
    scale_out = FF ** -0.5
    means_wide = jnp.swapaxes(weight_means, 1, 2)
    sigmas_wide = jnp.swapaxes(weight_sigmas, 1, 2)
    noise_wide = jnp.swapaxes(weight_noise, 1, 2)
    in_flip = to_sign(input_signs)
    out_flip = to_sign(jnp.transpose(output_signs, (2, 0, 1)))
    hid_flip = to_sign(hidden_signs.T)
    res_flip = to_sign(result_signs)
    perturb = (sigmas_wide.astype(jnp.float32) * noise_wide.astype(jnp.float32)).astype(jnp.bfloat16)
    flipped = (inputs.astype(jnp.float32) * in_flip).astype(jnp.bfloat16)
    gate = scale_in * jnp.dot(inputs, means_wide[0], preferred_element_type=jnp.float32) + scale_in * jnp.dot(flipped, perturb[0], preferred_element_type=jnp.float32) * out_flip[:, 0]
    up = scale_in * jnp.dot(inputs, means_wide[1], preferred_element_type=jnp.float32) + scale_in * jnp.dot(flipped, perturb[1], preferred_element_type=jnp.float32) * out_flip[:, 1]
    gate_sig = jax.nn.sigmoid(gate)
    hidden = (gate * gate_sig * up).astype(jnp.bfloat16)
    hid_flipped = (hidden.astype(jnp.float32) * hid_flip).astype(jnp.bfloat16)
    result = scale_out * jnp.dot(hidden, means_wide[2].T, preferred_element_type=jnp.float32) + scale_out * jnp.dot(hid_flipped, perturb[2].T, preferred_element_type=jnp.float32) * res_flip
    cot_flipped = (cotangent.astype(jnp.float32) * res_flip).astype(jnp.bfloat16)
    hid_grad = scale_out * jnp.dot(cotangent, means_wide[2], preferred_element_type=jnp.float32) + scale_out * jnp.dot(cot_flipped, perturb[2], preferred_element_type=jnp.float32) * hid_flip
    up_grad = (hid_grad * gate * gate_sig).astype(jnp.bfloat16)
    gate_grad = (hid_grad * up * gate_sig * (1.0 + gate * (1.0 - gate_sig))).astype(jnp.bfloat16)
    gate_flipped = (gate_grad.astype(jnp.float32) * out_flip[:, 0]).astype(jnp.bfloat16)
    up_flipped = (up_grad.astype(jnp.float32) * out_flip[:, 1]).astype(jnp.bfloat16)
    back_mean = jnp.dot(gate_grad, means_wide[0].T, preferred_element_type=jnp.float32) + jnp.dot(up_grad, means_wide[1].T, preferred_element_type=jnp.float32)
    back_pert = jnp.dot(gate_flipped, perturb[0].T, preferred_element_type=jnp.float32) + jnp.dot(up_flipped, perturb[1].T, preferred_element_type=jnp.float32)
    input_grad = scale_in * back_mean + scale_in * back_pert * in_flip
    mean_total = jnp.zeros((3, D, FF), jnp.float32)
    pert_total = jnp.zeros((3, D, FF), jnp.float32)
    for group in range(N_DP):
        lower = group * TOK_DEV
        upper = lower + TOK_DEV
        mean_terms = jnp.stack([
            scale_in * jnp.dot(inputs[lower:upper].T, gate_grad[lower:upper], preferred_element_type=jnp.float32),
            scale_in * jnp.dot(inputs[lower:upper].T, up_grad[lower:upper], preferred_element_type=jnp.float32),
            scale_out * jnp.dot(cotangent[lower:upper].T, hidden[lower:upper], preferred_element_type=jnp.float32)])
        pert_terms = jnp.stack([
            scale_in * jnp.dot(flipped[lower:upper].T, gate_flipped[lower:upper], preferred_element_type=jnp.float32),
            scale_in * jnp.dot(flipped[lower:upper].T, up_flipped[lower:upper], preferred_element_type=jnp.float32),
            scale_out * jnp.dot(cot_flipped[lower:upper].T, hid_flipped[lower:upper], preferred_element_type=jnp.float32)])
        mean_round = lax.optimization_barrier(mean_terms.astype(jnp.bfloat16))
        pert_round = lax.optimization_barrier(pert_terms.astype(jnp.bfloat16))
        mean_total = mean_total + mean_round.astype(jnp.float32)
        pert_total = pert_total + pert_round.astype(jnp.float32)
    mean_grad = jnp.swapaxes(mean_total.astype(jnp.bfloat16), 1, 2)
    sigma_grad = jnp.swapaxes((pert_total * noise_wide.astype(jnp.float32)).astype(jnp.bfloat16), 1, 2)
    return result.astype(jnp.bfloat16), input_grad.astype(jnp.bfloat16), mean_grad, sigma_grad
```

```python
import jax
import jax.numpy as jnp
from jax import lax
from jax.experimental import pallas as pl
from jax.experimental.pallas import tpu as pltpu
from jax.sharding import Mesh, PartitionSpec as P

D = 4096
FF = 14336
SCALE_IN = D ** (-0.5)
SCALE_OUT = FF ** (-0.5)
F = 224
T = 192
G = 4
PK = 336
CHIP = ("zl", "y", "x")
COLS = ("dp", "x", "c")
BF = jnp.bfloat16
F32 = jnp.float32


def a2a(x, axes):
    return lax.all_to_all(x, axes, split_axis=0, concat_axis=0, tiled=True)


def to_all(x, axes, n):
    return a2a(jnp.broadcast_to(x[None], (n, *x.shape)), axes)


def pack(v):
    rest = jnp.concatenate([v[: F // 2, 128:T], v[F // 2 :, 128:T]], axis=1)
    return jnp.concatenate([v[:, :128], rest], axis=0)


def unpack(v):
    rest = v[F:]
    return jnp.concatenate([v[:F], jnp.concatenate([rest[:, :64], rest[:, 64:]], axis=0)], axis=1)


def nt(a, b):
    return lax.dot_general(a, b, (((1,), (1,)), ((), ())), preferred_element_type=F32)


def tn(a, b):
    return lax.dot_general(a, b, (((0,), (0,)), ((), ())), preferred_element_type=F32)


def nn(a, b):
    return lax.dot_general(a, b, (((1,), (0,)), ((), ())), preferred_element_type=F32)


def rows_of(own, sib, which):
    parts = []
    for x in range(4):
        parts += [own[which, x, 0], sib[which, x, 0]]
    return jnp.concatenate(parts, axis=1)


def signed(a, b):
    return (a.astype(F32) * b.astype(F32)).astype(BF)


def weights_body(c_ref, m_ref, s_ref, n_ref, mo_ref, po_ref):
    c = c_ref[0]
    for x in range(4):
        for k in range(2):
            at = pl.multiple_of((2 * x + (c if k == 0 else 1 - c)) * 128, 128)
            to = pl.ds((2 * x + k) * 128, 128)
            mo_ref[0, :, to] = m_ref[0, :, pl.ds(at, 128)]
            po_ref[0, :, to] = signed(s_ref[0, :, pl.ds(at, 128)], n_ref[0, :, pl.ds(at, 128)])


def prepare_weights(c, means, sigmas, noise):
    spec = pl.BlockSpec((1, F, 1024), lambda i: (i, 0, 0))
    out = jax.ShapeDtypeStruct((3, F, 1024), BF)
    return pl.pallas_call(
        weights_body,
        grid=(3,),
        in_specs=[pl.BlockSpec(memory_space=pltpu.SMEM), spec, spec, spec],
        out_specs=[spec, spec],
        out_shape=[out, out],
        name="prepare_weights",
    )(c, means, sigmas, noise)


GATH = pl.BlockSpec((2, 4, 1, T, 128), lambda g: (0, 0, g, 0, 0))


def project_body(n, scale, own, sib, m_ref, p_ref, s_ref, o_ref):
    plain = rows_of(own, sib, 0)
    flip = signed(plain, rows_of(own, sib, 1))
    for k in range(n):
        mean = pack(nt(m_ref[k], plain))
        pert = pack(nt(p_ref[k], flip))
        sign = s_ref[0, k * PK : (k + 1) * PK].astype(F32)
        o_ref[0, k * PK : (k + 1) * PK] = (scale * mean + scale * pert * sign).astype(BF)


def project(own, sib, means, perturb, signs, first, n, scale, name):
    w = pl.BlockSpec((n, F, 1024), lambda g: (first // n, 0, 0))
    s = pl.BlockSpec((1, n * PK, 128), lambda g: (g, first // n, 0))
    return pl.pallas_call(
        lambda *refs: project_body(n, scale, *refs),
        grid=(G,),
        in_specs=[GATH, GATH, w, w, s],
        out_specs=pl.BlockSpec((1, n * PK, 128), lambda g: (g, 0, 0)),
        out_shape=jax.ShapeDtypeStruct((G, n * PK, 128), BF),
        name=name,
    )(own, sib, means, perturb, signs)


def pointwise_body(gu_ref, dh_ref, o_ref):
    def total(ref, k):
        v = ref[0, k * PK : (k + 1) * PK].astype(F32)
        for g in range(1, G):
            v = v + ref[g, k * PK : (k + 1) * PK].astype(F32)
        return v

    gate, up, dh = total(gu_ref, 0), total(gu_ref, 1), total(dh_ref, 0)
    sig = jax.nn.sigmoid(gate)
    o_ref[0:PK] = (gate * sig * up).astype(BF)
    o_ref[PK : 2 * PK] = (dh * up * sig * (1.0 + gate * (1.0 - sig))).astype(BF)
    o_ref[2 * PK :] = (dh * gate * sig).astype(BF)


def pointwise(gu, dh):
    return pl.pallas_call(
        pointwise_body, out_shape=jax.ShapeDtypeStruct((3 * PK, 128), BF), name="pointwise"
    )(gu, dh)


def back_body(n, first, scale, h_ref, s_ref, own, sib, m_ref, p_ref, oo_ref, os_ref):
    mean = pert = None
    for k in range(n):
        h = h_ref[0, k * PK : (k + 1) * PK]
        hb = signed(h, s_ref[0, k * PK : (k + 1) * PK])
        m, p = tn(unpack(h), m_ref[k]), tn(unpack(hb), p_ref[k])
        mean = m if mean is None else mean + m
        pert = p if pert is None else pert + p
    for x in range(4):
        for k, (o_ref, f_ref) in enumerate(((oo_ref, own), (os_ref, sib))):
            at = slice((2 * x + k) * 128, (2 * x + k + 1) * 128)
            sign = f_ref[0, x, 0].astype(F32)
            o_ref[x, 0] = (scale * mean[:, at] + scale * pert[:, at] * sign).astype(BF)


def back(h, signs, own, sib, means, perturb, first, n, scale, name):
    w = pl.BlockSpec((n, F, 1024), lambda g: (first // n, 0, 0))
    s = pl.BlockSpec((1, n * PK, 128), lambda g: (g, first // n, 0))
    hs = pl.BlockSpec((1, n * PK, 128), lambda g: (g, 0, 0))
    flip = pl.BlockSpec((1, 4, 1, T, 128), lambda g: (1, 0, g, 0, 0))
    o = pl.BlockSpec((4, 1, T, 128), lambda g: (0, g, 0, 0))
    out = jax.ShapeDtypeStruct((4, G, T, 128), BF)
    return pl.pallas_call(
        lambda *refs: back_body(n, first, scale, *refs),
        grid=(G,),
        in_specs=[hs, s, flip, flip, w, w],
        out_specs=[o, o],
        out_shape=[out, out],
        name=name,
    )(h, signs, own, sib, means, perturb)


def grads_body(c_ref, h_ref, gu_ref, s_ref, xo, xs, co, cs, n_ref, mo_ref, so_ref, lhs):
    c = c_ref[0]

    @pl.when(pl.program_id(0) == 0)
    def _():
        for g in range(G):
            for k in range(3):
                v = h_ref[g] if k == 2 else gu_ref[g, k * PK : (k + 1) * PK]
                lhs[2 * k, g] = unpack(v)
                lhs[2 * k + 1, g] = unpack(signed(v, s_ref[g, k * PK : (k + 1) * PK]))

    sums = [None] * 6
    for g in range(G):
        for first, ks, own, sib, scale in (
            (0, (0, 1), xo, xs, SCALE_IN),
            (2, (2,), co, cs, SCALE_OUT),
        ):
            plain = jnp.concatenate([own[0, 0, g], sib[0, 0, g]], axis=1)
            flip = signed(plain, jnp.concatenate([own[1, 0, g], sib[1, 0, g]], axis=1))
            for k in ks:
                for j, rhs in enumerate((plain, flip)):
                    term = (scale * nn(lhs[2 * k + j, g], rhs)).astype(BF).astype(F32)
                    at = 2 * k + j
                    sums[at] = term if sums[at] is None else sums[at] + term
    for k in range(3):
        for half in range(2):
            at = slice(half * 128, (half + 1) * 128)
            to = pl.ds(pl.multiple_of((c if half == 0 else 1 - c) * 128, 128), 128)
            mo_ref[k, :, to] = sums[2 * k][:, at].astype(BF)
            so_ref[k, :, to] = (sums[2 * k + 1][:, at] * n_ref[k, :, to].astype(F32)).astype(BF)


def grads(c, h, gu, signs, xo, xs, co, cs, noise):
    gath = pl.BlockSpec((2, 1, G, T, 128), lambda x: (0, x, 0, 0, 0))
    w = pl.BlockSpec((3, F, 256), lambda x: (0, 0, x))
    out = jax.ShapeDtypeStruct((3, F, 1024), BF)

    def whole(a):
        return pl.BlockSpec(a.shape, lambda x: (0,) * a.ndim)

    return pl.pallas_call(
        grads_body,
        grid=(4,),
        in_specs=[
            pl.BlockSpec(memory_space=pltpu.SMEM),
            whole(h),
            whole(gu),
            whole(signs),
            gath,
            gath,
            gath,
            gath,
            w,
        ],
        out_specs=[w, w],
        out_shape=[out, out],
        scratch_shapes=[pltpu.VMEM((6, G, F, T), BF)],
        name="grads",
    )(c, h, gu, signs, xo, xs, co, cs, noise)


def gather_chips(block):
    out = to_all(block, CHIP, 32).reshape(8, 4, 2, G, 24, 128)
    own = out.transpose(2, 1, 3, 0, 4, 5).reshape(2, 4, G, T, 128)
    own = lax.optimization_barrier(own)
    return own, lax.ppermute(own, "c", [(0, 1), (1, 0)])


def scatter_sum(own, sib):
    got = lax.ppermute(sib, "c", [(0, 1), (1, 0)])
    both = (own.astype(F32) + got.astype(F32)).astype(BF)
    both = both.reshape(4, G, 8, 24, 128).transpose(2, 0, 1, 3, 4).reshape(32, G * 24, 128)
    got = a2a(both, CHIP)
    return jnp.sum(got.astype(F32), axis=0).astype(BF)


def to_tokens(part):
    out = a2a(part.reshape(32, 3, 128), COLS)
    return out.transpose(1, 0, 2).reshape(3, D)


def to_sign(values):
    return (2 * values - 1).astype(BF)


def packed_signs(values):
    return pack(to_sign(values))


def on_device(
    inputs,
    weight_means,
    weight_sigmas,
    weight_noise,
    input_signs,
    output_signs,
    hidden_signs,
    result_signs,
    cotangent,
):
    c = lax.axis_index("c").reshape(1).astype(jnp.int32)
    mine = jnp.stack([inputs, to_sign(input_signs), cotangent, to_sign(result_signs)])
    mine = mine.reshape(4, 3, 32, 128).transpose(2, 0, 1, 3).reshape(32, 12, 128)
    cols = a2a(mine, COLS)
    cols = cols.reshape(G, 8, 4, 3, 128).transpose(2, 0, 1, 3, 4).reshape(4, G, 24, 128)
    signs = jnp.concatenate([packed_signs(output_signs[0]), packed_signs(output_signs[1]), packed_signs(hidden_signs)])
    cols, signs = lax.optimization_barrier((cols, signs))
    signs = to_all(signs, "dp", G)
    xo, xs = gather_chips(cols[:2])
    co, cs = gather_chips(cols[2:])
    means, perturb = prepare_weights(c, weight_means, weight_sigmas, weight_noise)
    gu = project(xo, xs, means, perturb, signs, 0, 2, SCALE_IN, "project_in")
    gu = a2a(gu, "dp")
    dh = project(co, cs, means, perturb, signs, 2, 1, SCALE_OUT, "project_cot")
    dh = a2a(dh, "dp")
    acts = pointwise(gu, dh)
    h = to_all(acts[:PK], "dp", G)
    gu_g = to_all(acts[PK:], "dp", G)
    ro, rs = back(h, signs, co, cs, means, perturb, 2, 1, SCALE_OUT, "back_result")
    result = to_tokens(scatter_sum(ro, rs))
    io, is_ = back(gu_g, signs, xo, xs, means, perturb, 0, 2, SCALE_IN, "back_input")
    input_grad = to_tokens(scatter_sum(io, is_))
    mean_grad, sigma_grad = grads(c, h, gu_g, signs, xo, xs, co, cs, weight_noise)
    return result, input_grad, mean_grad, sigma_grad


def solution(mesh):
    fine = Mesh(mesh.devices.reshape(4, 2, 4, 4, 2), ("dp", "zl", "y", "x", "c"))
    tok = P(("dp", "zl", "y", "x", "c"), None)
    ff = ("zl", "y", "x", "c")
    wide = P(None, ff, "dp")
    return jax.shard_map(
        on_device,
        mesh=fine,
        in_specs=(tok, wide, wide, wide, tok, wide, P(ff, "dp"), tok, tok),
        out_specs=(tok, tok, wide, wide),
        check_vma=False,
    )
```

```python
import jax
import jax.numpy as jnp
from jax import lax
from jax.experimental import pallas as pl
from jax.experimental.pallas import tpu as pltpu
from jax.sharding import Mesh, PartitionSpec as P


D = 4096
FF = 14336
SCALE_IN = D ** (-0.5)
SCALE_OUT = FF ** (-0.5)
F = 224
W = 1024
T = 192
G = 4
PK = 336
CHIP = ("zl", "y", "x")
COLS = ("dp", "x", "c")
SWAP = [(0, 1), (1, 0)]
BF = jnp.bfloat16
F32 = jnp.float32


def a2a(x, axes):
    return lax.all_to_all(x, axes, split_axis=0, concat_axis=0, tiled=True)


def shift(x, axis, by):
    return lax.ppermute(x, axis, [(i, (i + by) % 4) for i in range(4)])


def ring(block, axis):
    half = block.shape[0] // 2
    below, above = shift(block, axis, 1), shift(block, axis, -1)
    return below, above, shift(below[:half], axis, 1), shift(above[half:], axis, -1)


def pack(v):
    rest = jnp.concatenate([v[: F // 2, 128:T], v[F // 2 :, 128:T]], axis=1)
    return jnp.concatenate([v[:, :128], rest], axis=0)


def unpack(v):
    rest = v[F:]
    return jnp.concatenate([v[:F], jnp.concatenate([rest[:, :64], rest[:, 64:]], axis=0)], axis=1)


def nt(a, b):
    return lax.dot_general(a, b, (((1,), (1,)), ((), ())), preferred_element_type=F32)


def tn(a, b):
    return lax.dot_general(a, b, (((0,), (0,)), ((), ())), preferred_element_type=F32)


def nn(a, b):
    return lax.dot_general(a, b, (((1,), (0,)), ((), ())), preferred_element_type=F32)


ON_CHIP = pl.BlockSpec(memory_space=pltpu.VMEM)
SCALARS = pl.BlockSpec(memory_space=pltpu.SMEM)


def on_chip_call(body, args, out, scratch=(), mib=16, flops=0):
    moved = sum(a.size for a in args[1:]) * 2
    return pl.pallas_call(
        body,
        in_specs=[SCALARS] + [ON_CHIP] * (len(args) - 1),
        out_specs=[ON_CHIP] * len(out),
        out_shape=[jax.ShapeDtypeStruct(o, BF) for o in out],
        scratch_shapes=list(scratch),
        compiler_params=pltpu.CompilerParams(vmem_limit_bytes=mib * 1024 * 1024),
        cost_estimate=pl.CostEstimate(flops=flops, bytes_accessed=moved, transcendentals=0),
    )(*args)


def perturb_body(s_ref, n_ref, o_ref):
    o_ref[...] = (s_ref[...].astype(F32) * n_ref[...].astype(F32)).astype(BF)


def perturbation(sigmas, noise):
    spec = pl.BlockSpec((1, F, W), lambda i: (i, 0, 0))
    return pl.pallas_call(
        perturb_body,
        grid=(3,),
        in_specs=[spec, spec],
        out_specs=spec,
        out_shape=jax.ShapeDtypeStruct((3, F, W), BF),
        name="perturbation",
    )(sigmas, noise)


def assemble_body(by_y, pos, *refs):
    pieces, (plain_ref, sign_ref, both) = refs[:10], refs[10:]
    zl, y, x, c = pos[1], pos[2], pos[3], pos[4]

    def one_group(g, carry):
        for k in range(2):
            col = c if k == 0 else 1 - c
            for j, (outer, first, count) in enumerate(
                ((0, 0, 4), (1, 0, 4), (3, 0, 4), (2, 0, 2), (2, 2, 2))
            ):
                ref = pieces[5 * k + j]
                for i in range(count):
                    dy, dx = (outer, first + i) if by_y else (first + i, outer)
                    lane = (2 * ((x + dx) & 3) + col) * 128
                    for z in range(2):
                        row = (zl if z == 0 else 1 - zl) * 4 + ((y + dy) & 3)
                        for a in range(2):
                            at = pl.ds(pl.multiple_of(lane, 128), 128)
                            both[a, row, :, at] = ref[i, z, a, g].astype(F32)
        plain_ref[g] = both[0].reshape(T, W).astype(BF)
        sign_ref[g] = both[1].reshape(T, W).astype(BF)
        return carry

    lax.fori_loop(0, G, one_group, 0)


def assemble(pos, pieces, by_y):
    return on_chip_call(
        lambda *refs: assemble_body(by_y, *refs),
        [pos, *pieces],
        [(G, T, W)] * 2,
        scratch=[pltpu.VMEM((2, 8, 24, W), F32)],
    )


def gather(block, inner, outer):
    both = jnp.stack([block, lax.ppermute(block, "zl", SWAP)])
    line = jnp.stack([both, shift(both, inner, -1), shift(both, inner, 2), shift(both, inner, 1)])
    below, above, first, second = ring(line, outer)
    own = [line, above, below, first, second]
    return own + [lax.ppermute(p, "c", SWAP) for p in own]


def project_body(rels, pos, x_ref, a_ref, t_ref, r_ref, m_ref, p_ref, s_ref, o_ref):
    def one_group(i, carry):
        rel = rels[0] + i * (rels[1] - rels[0]) if len(rels) > 1 else rels[0]
        g = (pos[0] + rel) & 3
        x, cot = x_ref[g], t_ref[g]
        xa, cr = x * a_ref[g], cot * r_ref[g]
        for k, (plain, flip, scale) in enumerate(
            ((x, xa, SCALE_IN), (x, xa, SCALE_IN), (cot, cr, SCALE_OUT))
        ):
            at = slice(k * PK, (k + 1) * PK)
            mean = pack(nt(m_ref[k], plain))
            pert = pack(nt(p_ref[k], flip))
            sign = s_ref[rel, at].astype(F32)
            o_ref[i, at] = (scale * mean + scale * pert * sign).astype(BF)
        return carry

    lax.fori_loop(0, len(rels), one_group, 0)


def project(pos, acts, means, perturb, signs, rels):
    return on_chip_call(
        lambda *refs: project_body(rels, *refs),
        [pos, *acts, means, perturb, signs],
        [(len(rels), 3 * PK, 128)],
        flops=len(rels) * 12 * F * W * T,
    )[0]


def pointwise_body(a_ref, b_ref, c_ref, o_ref):
    def total(k):
        at = slice(k * PK, (k + 1) * PK)
        return a_ref[at].astype(F32) + b_ref[at].astype(F32) + c_ref[at].astype(F32)

    gate, up, dh = total(0), total(1), total(2)
    sig = jax.nn.sigmoid(gate)
    o_ref[0:PK] = (dh * up * sig * (1.0 + gate * (1.0 - sig))).astype(BF)
    o_ref[PK : 2 * PK] = (dh * gate * sig).astype(BF)
    o_ref[2 * PK :] = (gate * sig * up).astype(BF)


def pointwise(pos, a, b, c):
    return on_chip_call(lambda _, *refs: pointwise_body(*refs), [pos, a, b, c], [(3 * PK, 128)])[0]


def back_body(rels, pos, h_ref, s_ref, a_ref, r_ref, m_ref, p_ref, o_ref):
    c = pos[4]

    def one_group(i, carry):
        rel = rels[0] + i * (rels[1] - rels[0]) if len(rels) > 1 else rels[0]
        g = (pos[0] + rel) & 3

        def pair(k):
            at = slice(k * PK, (k + 1) * PK)
            h = h_ref[i, at]
            return tn(unpack(h), m_ref[k]), tn(unpack(h * s_ref[rel, at]), p_ref[k])

        rm, rp = pair(2)
        gm, gp = pair(0)
        um, up = pair(1)
        for j, (mean, pert, sign, scale) in enumerate(
            ((rm, rp, r_ref, SCALE_OUT), (gm + um, gp + up, a_ref, SCALE_IN))
        ):
            v = (scale * mean + scale * pert * sign[g].astype(F32)).astype(BF)
            for col in range(2):
                for x in range(4):
                    at = (2 * x + col) * 128
                    o_ref[c if col == 0 else 1 - c, i, j, x] = v[:, at : at + 128]
        return carry

    lax.fori_loop(0, len(rels), one_group, 0)


def back(pos, h, signs, a, r, means, perturb, rels):
    return on_chip_call(
        lambda *refs: back_body(rels, *refs),
        [pos, h, signs, a, r, means, perturb],
        [(2, len(rels), 2, 4, T, 128)],
        flops=len(rels) * 12 * F * W * T,
    )[0]


def grads_body(pos, h0, h13, h2, s_ref, x_ref, a_ref, t_ref, r_ref, n_ref, mo_ref, so_ref, lhs):
    @pl.when(pl.program_id(0) == 0)
    def _():
        for rel, (ref, i) in enumerate(((h0, 0), (h13, 0), (h2, 0), (h13, 1))):
            for k in range(3):
                v = ref[i, k * PK : (k + 1) * PK]
                lhs[2 * k, rel] = unpack(v)
                lhs[2 * k + 1, rel] = unpack(v * s_ref[rel, k * PK : (k + 1) * PK])

    sums = [None] * 6
    for rel in range(G):
        g = (pos[0] + rel) & 3
        for ks, plain_ref, sign_ref, scale in (
            ((0, 1), x_ref, a_ref, SCALE_IN),
            ((2,), t_ref, r_ref, SCALE_OUT),
        ):
            plain = plain_ref[g]
            flip = plain * sign_ref[g]
            for k in ks:
                for j, rhs in enumerate((plain, flip)):
                    term = (scale * nn(lhs[2 * k + j, rel], rhs)).astype(BF).astype(F32)
                    at = 2 * k + j
                    sums[at] = term if sums[at] is None else sums[at] + term
    for k in range(3):
        mo_ref[k] = sums[2 * k].astype(BF)
        so_ref[k] = (sums[2 * k + 1] * n_ref[k].astype(F32)).astype(BF)


def grads(pos, h0, h13, h2, signs, acts, noise):
    w = pl.BlockSpec((3, F, 256), lambda i: (0, 0, i))
    group = pl.BlockSpec((G, T, 256), lambda i: (0, 0, i))
    out = jax.ShapeDtypeStruct((3, F, W), BF)
    return pl.pallas_call(
        grads_body,
        grid=(4,),
        in_specs=[SCALARS] + [ON_CHIP] * 4 + [group] * 4 + [w],
        out_specs=[w, w],
        scratch_shapes=[pltpu.VMEM((6, G, F, T), BF)],
        out_shape=[out, out],
        compiler_params=pltpu.CompilerParams(vmem_limit_bytes=28 * 1024 * 1024),
        cost_estimate=pl.CostEstimate(
            flops=48 * F * W * T, bytes_accessed=8 * G * T * W + 18 * F * W, transcendentals=0
        ),
        name="grads",
    )(pos, h0, h13, h2, signs, *acts, noise)


def merged(out):
    return (out[0].astype(F32) + lax.ppermute(out[1], "c", SWAP).astype(F32)).astype(BF)


def to_sign(values):
    return (2 * values - 1).astype(BF)


def packed_signs(values):
    return pack(to_sign(values))


def on_device(
    inputs,
    weight_means,
    weight_sigmas,
    weight_noise,
    input_signs,
    output_signs,
    hidden_signs,
    result_signs,
    cotangent,
):
    place = [lax.axis_index(name) for name in ("dp", "zl", "y", "x", "c")]
    pos = jnp.stack(place).astype(jnp.int32)
    mine = jnp.stack([inputs, to_sign(input_signs), cotangent, to_sign(result_signs)])
    mine = mine.reshape(4, 3, 32, 128).transpose(2, 0, 1, 3).reshape(32, 12, 128)
    cols = a2a(mine, COLS)
    cols = cols.reshape(G, 8, 4, 3, 128).transpose(2, 0, 1, 3, 4).reshape(4, G, 24, 128)
    signs = jnp.concatenate(
        [packed_signs(output_signs[0]), packed_signs(output_signs[1]), packed_signs(hidden_signs)]
    )
    cols, signs = lax.optimization_barrier((cols, signs))
    xs = gather(cols[:2], "x", "y")
    cs = gather(cols[2:], "y", "x")
    below, above, first, second = ring(signs, "dp")
    signs = jnp.stack([signs, above, jnp.concatenate([first, second]), below])
    perturb = perturbation(weight_sigmas, weight_noise)
    x, a = assemble(pos, xs, True)
    t, r = assemble(pos, cs, False)
    acts = (x, a, t, r)

    half = 3 * PK // 2
    far = project(pos, acts, weight_means, perturb, signs, (2,))[0]
    from_below = shift(far[:half], "dp", 1)
    from_above = shift(far[half:], "dp", -1)
    near = project(pos, acts, weight_means, perturb, signs, (1, 3))

    def plus(u, v):
        return (u.astype(F32) + v.astype(F32)).astype(BF)

    up = jnp.concatenate([plus(near[0, :half], from_below), near[0, half:]])
    down = jnp.concatenate([near[1, :half], plus(near[1, half:], from_above)])
    up, down = shift(up, "dp", 1), shift(down, "dp", -1)
    own = project(pos, acts, weight_means, perturb, signs, (0,))[0]
    h = pointwise(pos, own, up, down)

    below, above, first, second = ring(h, "dp")
    h0 = h[None]
    h13 = jnp.stack([above, below])
    h2 = jnp.concatenate([first, second])[None]
    outs = []
    for hs, rels in ((h0, (0,)), (h13, (1, 3)), (h2, (2,))):
        outs.append(merged(back(pos, hs, signs, a, r, weight_means, perturb, rels)))
    both = jnp.stack([outs[0][0], outs[1][0], outs[2][0], outs[1][1]])
    both = both.reshape(G, 2, 4, 8, 24, 128).transpose(3, 2, 0, 1, 4, 5).reshape(32, 8 * 24, 128)
    got = a2a(both, CHIP)
    mean_grad, sigma_grad = grads(pos, h0, h13, h2, signs, acts, weight_noise)
    got = jnp.sum(got.astype(F32), axis=0).astype(BF)
    got = got.reshape(G, 2, 8, 3, 128)
    got = lax.dynamic_slice_in_dim(jnp.concatenate([got, got]), (4 - place[0]) % 4, G, axis=0)
    got = got.transpose(0, 2, 1, 3, 4).reshape(32, 6, 128)
    got = a2a(got, COLS).reshape(32, 2, 3, 128).transpose(1, 2, 0, 3).reshape(2, 3, D)
    return got[0], got[1], mean_grad, sigma_grad


def solution(mesh):
    fine = Mesh(mesh.devices.reshape(4, 2, 4, 4, 2), ("dp", "zl", "y", "x", "c"))
    tok = P(("dp", "zl", "y", "x", "c"), None)
    ff = ("zl", "y", "x", "c")
    wide = P(None, ff, "dp")

    return jax.shard_map(
        on_device,
        mesh=fine,
        in_specs=(tok, wide, wide, wide, tok, wide, P(ff, "dp"), tok, tok),
        out_specs=(tok, tok, wide, wide),
        check_vma=False,
    )
```

```python
import jax
import jax.numpy as jnp
from jax import lax
from jax.experimental import pallas as pl
from jax.experimental.pallas import tpu as pltpu
from jax.sharding import Mesh, PartitionSpec as P


D = 4096
FF = 14336
SCALE_IN = D ** (-0.5)
SCALE_OUT = FF ** (-0.5)
F = 224
W = 1024
T = 192
G = 4
PK = 336
CHIP = ("zl", "y", "x")
ROWS = T * 8
SWAP = [(0, 1), (1, 0)]
BF = jnp.bfloat16
F32 = jnp.float32


def a2a(x, axes):
    return lax.all_to_all(x, axes, split_axis=0, concat_axis=0, tiled=True)


def shift(x, axis, by):
    return lax.ppermute(x, axis, [(i, (i + by) % 4) for i in range(4)])


def ring(block, axis):
    half = block.shape[0] // 2
    below, above = shift(block, axis, 1), shift(block, axis, -1)
    return below, above, shift(below[:half], axis, 1), shift(above[half:], axis, -1)


def pack(v):
    rest = jnp.concatenate([v[: F // 2, 128:T], v[F // 2 :, 128:T]], axis=1)
    return jnp.concatenate([v[:, :128], rest], axis=0)


def unpack(v):
    rest = v[F:]
    return jnp.concatenate([v[:F], jnp.concatenate([rest[:, :64], rest[:, 64:]], axis=0)], axis=1)


def nt(a, b):
    return lax.dot_general(a, b, (((1,), (1,)), ((), ())), preferred_element_type=F32)


def tn(a, b):
    return lax.dot_general(a, b, (((0,), (0,)), ((), ())), preferred_element_type=F32)


def nn(a, b):
    return lax.dot_general(a, b, (((1,), (0,)), ((), ())), preferred_element_type=F32)


ON_CHIP = pl.BlockSpec(memory_space=pltpu.VMEM)
SCALARS = pl.BlockSpec(memory_space=pltpu.SMEM)


def on_chip_call(body, args, out, scratch=(), mib=16, flops=0):
    moved = sum(a.size for a in args[1:]) * 2
    return pl.pallas_call(
        body,
        in_specs=[SCALARS] + [ON_CHIP] * (len(args) - 1),
        out_specs=[ON_CHIP] * len(out),
        out_shape=[jax.ShapeDtypeStruct(o, BF) for o in out],
        scratch_shapes=list(scratch),
        compiler_params=pltpu.CompilerParams(vmem_limit_bytes=mib * 1024 * 1024),
        cost_estimate=pl.CostEstimate(flops=flops, bytes_accessed=moved, transcendentals=0),
    )(*args)


def as_sign(values):
    return (2 * values - 1).astype(F32)


def prepare_body(pos, x_ref, a_ref, t_ref, r_ref, cols_ref, rows):
    for k, v in enumerate(
        (x_ref[...].astype(F32), as_sign(a_ref[...]), t_ref[...].astype(F32), as_sign(r_ref[...]))
    ):
        for d in range(G):
            rel = (d - pos[0]) & 3
            for j in range(8):
                at = (8 * d + j) * 128
                rows[rel, k, pl.ds(j, 3, stride=8)] = v[:, at : at + 128]
    cols_ref[...] = rows[...].astype(BF)


def prepare(*args):
    return on_chip_call(
        prepare_body, args, [(G, 4, 24, 128)], scratch=[pltpu.VMEM((G, 4, 24, 128), F32)]
    )[0]


def signs_body(_, s_ref, h_ref, o_ref):
    for k in range(3):
        v = s_ref[k] if k < 2 else h_ref[...]
        o_ref[k * PK : (k + 1) * PK] = pack(as_sign(v)).astype(BF)


def packed_signs(*args):
    return on_chip_call(signs_body, args, [(3 * PK, 128)])[0]


def finish_body(pos, p0, p1, p2, p3, res_ref, inp_ref, rows):
    for j, ref in enumerate((p0, p1, p2, p3)):
        rows[(pos[0] + j) & 3] = ref[...].astype(F32)
    for k, o_ref in enumerate((res_ref, inp_ref)):
        for d in range(G):
            for j in range(8):
                at = (8 * d + j) * 128
                o_ref[:, at : at + 128] = rows[d, pl.ds(24 * k + j, 3, stride=8)].astype(BF)


def finish(*args):
    return on_chip_call(
        finish_body, args, [(3, D), (3, D)], scratch=[pltpu.VMEM((G, 48, 128), F32)]
    )


def perturb_body(s_ref, n_ref, o_ref):
    o_ref[...] = (s_ref[...].astype(F32) * n_ref[...].astype(F32)).astype(BF)


def perturbation(sigmas, noise):
    spec = pl.BlockSpec((1, F, W), lambda i: (i, 0, 0))
    return pl.pallas_call(
        perturb_body,
        grid=(3,),
        in_specs=[spec, spec],
        out_specs=spec,
        out_shape=jax.ShapeDtypeStruct((3, F, W), BF),
        compiler_params=pltpu.CompilerParams(vmem_limit_bytes=8 * 1024 * 1024),
        name="perturbation",
    )(sigmas, noise)


def assemble_body(by_y, pos, *refs):
    pieces, (plain_ref, sign_ref, both) = refs[:8], refs[8:]
    zl, y, x, c = pos[1], pos[2], pos[3], pos[4]

    def one_group(g, carry):
        for k in range(2):
            col = c if k == 0 else 1 - c
            for outer in range(4):
                ref = pieces[4 * k + outer]
                for i in range(4):
                    dy, dx = (outer, i) if by_y else (i, outer)
                    my = 2 * ((x + dx) & 3) + col
                    for z in range(2):
                        mx = (zl if z == 0 else 1 - zl) * 4 + ((y + dy) & 3)
                        at = pl.ds(pl.multiple_of((mx * 8 + my) * 24, 8), 24)
                        for a in range(2):
                            both[a, at] = ref[i, z, a, g].astype(F32)
        for a, o_ref in ((0, plain_ref), (1, sign_ref)):
            for j in range(8):
                o_ref[g, :, j * 128 : (j + 1) * 128] = both[a, pl.ds(j, T, stride=8)].astype(BF)
        return carry

    lax.fori_loop(0, G, one_group, 0)


def assemble(pos, pieces, by_y):
    return on_chip_call(
        lambda *refs: assemble_body(by_y, *refs),
        [pos, *pieces],
        [(G, T, W)] * 2,
        scratch=[pltpu.VMEM((2, ROWS, 128), F32)],
    )


def gather(both, inner, outer):
    line = jnp.stack([both, shift(both, inner, -1), shift(both, inner, 2), shift(both, inner, 1)])
    below, above = shift(line, outer, 1), shift(line, outer, -1)
    own = [line, above, shift(below, outer, 1), below]
    return own + [lax.ppermute(p, "c", SWAP) for p in own]


def project_body(rels, pos, x_ref, a_ref, t_ref, r_ref, m_ref, p_ref, *refs):
    s_refs, o_ref = refs[:-1], refs[-1]
    for i, rel in enumerate(rels):
        x, cot = x_ref[rel], t_ref[rel]
        xa, cr = x * a_ref[rel], cot * r_ref[rel]
        for k, (plain, flip, scale) in enumerate(
            ((x, xa, SCALE_IN), (x, xa, SCALE_IN), (cot, cr, SCALE_OUT))
        ):
            at = slice(k * PK, (k + 1) * PK)
            mean = pack(nt(m_ref[k], plain))
            pert = pack(nt(p_ref[k], flip))
            o_ref[i, at] = (scale * mean + scale * pert * s_refs[i][at].astype(F32)).astype(BF)


def project(pos, acts, means, perturb, signs, rels):
    return on_chip_call(
        lambda *refs: project_body(rels, *refs),
        [pos, *acts, means, perturb, *(signs[rel] for rel in rels)],
        [(len(rels), 3 * PK, 128)],
        flops=len(rels) * 12 * F * W * T,
    )[0]


def pointwise_body(a_ref, b_ref, c_ref, o_ref):
    def total(k):
        at = slice(k * PK, (k + 1) * PK)
        return a_ref[at].astype(F32) + b_ref[at].astype(F32) + c_ref[at].astype(F32)

    gate, up, dh = total(0), total(1), total(2)
    sig = jax.nn.sigmoid(gate)
    o_ref[0:PK] = (dh * up * sig * (1.0 + gate * (1.0 - sig))).astype(BF)
    o_ref[PK : 2 * PK] = (dh * gate * sig).astype(BF)
    o_ref[2 * PK :] = (gate * sig * up).astype(BF)


def pointwise(pos, a, b, c):
    return on_chip_call(lambda _, *refs: pointwise_body(*refs), [pos, a, b, c], [(3 * PK, 128)])[0]


def back_body(rels, pos, a_ref, r_ref, m_ref, p_ref, *refs):
    n = len(rels)
    h_refs, s_refs, o_ref, rows = refs[:n], refs[n : 2 * n], refs[2 * n], refs[2 * n + 1]
    c = pos[4]
    for i, rel in enumerate(rels):

        def pair(k):
            at = slice(k * PK, (k + 1) * PK)
            h = h_refs[i][at]
            return tn(unpack(h), m_ref[k]), tn(unpack(h * s_refs[i][at]), p_ref[k])

        rm, rp = pair(2)
        gm, gp = pair(0)
        um, up = pair(1)
        for j, (mean, pert, sign, scale) in enumerate(
            ((rm, rp, r_ref, SCALE_OUT), (gm + um, gp + up, a_ref, SCALE_IN))
        ):
            v = scale * mean + scale * pert * sign[rel].astype(F32)
            for k in range(8):
                rows[pl.ds(k, T, stride=8)] = v[:, k * 128 : (k + 1) * 128]
            for col in range(2):
                half = c if col == 0 else 1 - c

                def place(q, carry):
                    at = pl.multiple_of(q * 48 + col * 24, 8)
                    o_ref[half, q, i, j] = rows[pl.ds(at, 24)].astype(BF)
                    return carry

                lax.fori_loop(0, 32, place, 0, unroll=4)


def back(pos, h, signs, a, r, means, perturb, rels):
    return on_chip_call(
        lambda *refs: back_body(rels, *refs),
        [pos, a, r, means, perturb, *h, *(signs[rel] for rel in rels)],
        [(2, 32, len(rels), 2, 24, 128)],
        scratch=[pltpu.VMEM((ROWS, 128), F32)],
        flops=len(rels) * 12 * F * W * T,
    )[0]


def grads_body(*refs):
    hs, signs = refs[:4], refs[4:8]
    x_ref, a_ref, t_ref, r_ref, n_ref, mo_ref, so_ref, lhs, sums = refs[8:]

    @pl.when(pl.program_id(0) == 0)
    def _():
        for rel in range(G):
            for k in range(3):
                v = hs[rel][k * PK : (k + 1) * PK]
                lhs[rel, 2 * k] = unpack(v)
                lhs[rel, 2 * k + 1] = unpack(v * signs[rel][k * PK : (k + 1) * PK])

    sums[...] = jnp.zeros(sums.shape, F32)

    def one_group(rel, carry):
        x, cot = x_ref[rel], t_ref[rel]
        for k, (plain, sign_ref, scale) in enumerate(
            ((x, a_ref, SCALE_IN), (x, a_ref, SCALE_IN), (cot, r_ref, SCALE_OUT))
        ):
            for j, rhs in enumerate((plain, plain * sign_ref[rel])):
                at = 2 * k + j
                sums[at] += (scale * nn(lhs[rel, at], rhs)).astype(BF).astype(F32)
        return carry

    lax.fori_loop(0, G, one_group, 0)
    for k in range(3):
        mo_ref[k] = sums[2 * k].astype(BF)
        so_ref[k] = (sums[2 * k + 1] * n_ref[k].astype(F32)).astype(BF)


def grads(h, signs, acts, noise):
    w = pl.BlockSpec((3, F, 256), lambda i: (0, 0, i))
    group = pl.BlockSpec((G, T, 256), lambda i: (0, 0, i))
    out = jax.ShapeDtypeStruct((3, F, W), BF)
    return pl.pallas_call(
        grads_body,
        grid=(4,),
        in_specs=[ON_CHIP] * 8 + [group] * 4 + [w],
        out_specs=[w, w],
        scratch_shapes=[pltpu.VMEM((G, 6, F, T), BF), pltpu.VMEM((6, F, 256), F32)],
        out_shape=[out, out],
        compiler_params=pltpu.CompilerParams(vmem_limit_bytes=28 * 1024 * 1024),
        cost_estimate=pl.CostEstimate(
            flops=48 * F * W * T, bytes_accessed=8 * G * T * W + 18 * F * W, transcendentals=0
        ),
        name="grads",
    )(*h, *signs, *acts, noise)


def merged(out):
    return (out[0].astype(F32) + lax.ppermute(out[1], "c", SWAP).astype(F32)).astype(BF)


def over_dp(rel):
    return [rel[0]] + [shift(rel[4 - j], "dp", 4 - j) for j in range(1, 4)]


def on_device(
    inputs,
    weight_means,
    weight_sigmas,
    weight_noise,
    input_signs,
    output_signs,
    hidden_signs,
    result_signs,
    cotangent,
):
    place = [lax.axis_index(name) for name in ("dp", "zl", "y", "x", "c")]
    pos = jnp.stack(place).astype(jnp.int32)
    cols = over_dp(prepare(pos, inputs, input_signs, cotangent, result_signs))
    perturb = perturbation(weight_sigmas, weight_noise)
    cols = jnp.stack(cols, axis=1)
    cols = jnp.stack([cols, lax.ppermute(cols, "zl", SWAP)])
    signs = packed_signs(pos, output_signs, hidden_signs)
    signs = [signs] + [shift(signs, "dp", 4 - j) for j in range(1, 4)]
    xs = gather(cols[:, :2], "x", "y")
    cs = gather(cols[:, 2:], "y", "x")
    x, a = assemble(pos, xs, True)
    t, r = assemble(pos, cs, False)
    acts = (x, a, t, r)

    half = 3 * PK // 2
    far = project(pos, acts, weight_means, perturb, signs, (2,))[0]
    from_below = shift(far[:half], "dp", 1)
    from_above = shift(far[half:], "dp", -1)
    near = project(pos, acts, weight_means, perturb, signs, (1, 3))

    def plus(u, v):
        return (u.astype(F32) + v.astype(F32)).astype(BF)

    up = jnp.concatenate([plus(near[0, :half], from_below), near[0, half:]])
    down = jnp.concatenate([near[1, :half], plus(near[1, half:], from_above)])
    up, down = shift(up, "dp", 1), shift(down, "dp", -1)
    own = project(pos, acts, weight_means, perturb, signs, (0,))[0]
    h = pointwise(pos, own, up, down)

    below, above, first, second = ring(h, "dp")
    h = [h, above, jnp.concatenate([first, second]), below]
    outs = []
    for rels in ((0,), (1, 3), (2,)):
        outs.append(merged(back(pos, [h[j] for j in rels], signs, a, r, weight_means, perturb, rels)))
    got = jnp.concatenate(outs, axis=1).reshape(32, 192, 128)
    got = a2a(got, CHIP)
    mean_grad, sigma_grad = grads(h, signs, acts, weight_noise)
    got = jnp.sum(got.astype(F32), axis=0).astype(BF)
    got = over_dp([got[:48], got[48:96], got[144:], got[96:144]])
    result, input_grad = finish(pos, *got)
    return result, input_grad, mean_grad, sigma_grad


def solution(mesh):
    fine = Mesh(mesh.devices.reshape(4, 2, 4, 4, 2), ("dp", "zl", "y", "x", "c"))
    tok = P(("dp", "zl", "y", "x", "c"), None)
    ff = ("zl", "y", "x", "c")
    wide = P(None, ff, "dp")

    return jax.shard_map(
        on_device,
        mesh=fine,
        in_specs=(tok, wide, wide, wide, tok, wide, P(ff, "dp"), tok, tok),
        out_specs=(tok, tok, wide, wide),
        check_vma=False,
    )
```

```python
import jax
import jax.numpy as jnp
from jax import lax
from jax.experimental import pallas as pl
from jax.experimental.pallas import tpu as pltpu
from jax.sharding import Mesh, PartitionSpec as P


D = 4096
FF = 14336
SCALE_IN = D ** (-0.5)
SCALE_OUT = FF ** (-0.5)
F = 224
W = 1024
T = 192
G = 4
PK = 336
CHIP = ("zl", "y", "x")
ROWS = T * 8
SWAP = [(0, 1), (1, 0)]
BF = jnp.bfloat16
F32 = jnp.float32


def a2a(x, axes):
    return lax.all_to_all(x, axes, split_axis=0, concat_axis=0, tiled=True)


def shift(x, axis, by):
    return lax.ppermute(x, axis, [(i, (i + by) % 4) for i in range(4)])


def ring(block, axis):
    half = block.shape[0] // 2
    below, above = shift(block, axis, 1), shift(block, axis, -1)
    return below, above, shift(below[:half], axis, 1), shift(above[half:], axis, -1)


def pack(v):
    rest = jnp.concatenate([v[: F // 2, 128:T], v[F // 2 :, 128:T]], axis=1)
    return jnp.concatenate([v[:, :128], rest], axis=0)


def unpack(v):
    rest = v[F:]
    return jnp.concatenate([v[:F], jnp.concatenate([rest[:, :64], rest[:, 64:]], axis=0)], axis=1)


def nt(a, b):
    return lax.dot_general(a, b, (((1,), (1,)), ((), ())), preferred_element_type=F32)


def tn(a, b):
    return lax.dot_general(a, b, (((0,), (0,)), ((), ())), preferred_element_type=F32)


def nn(a, b):
    return lax.dot_general(a, b, (((1,), (0,)), ((), ())), preferred_element_type=F32)


ON_CHIP = pl.BlockSpec(memory_space=pltpu.VMEM)
SCALARS = pl.BlockSpec(memory_space=pltpu.SMEM)


def on_chip_call(body, args, out, scratch=(), mib=16, flops=0):
    moved = sum(a.size for a in args[1:]) * 2
    return pl.pallas_call(
        body,
        in_specs=[SCALARS] + [ON_CHIP] * (len(args) - 1),
        out_specs=[ON_CHIP] * len(out),
        out_shape=[jax.ShapeDtypeStruct(o, BF) for o in out],
        scratch_shapes=list(scratch),
        compiler_params=pltpu.CompilerParams(vmem_limit_bytes=mib * 1024 * 1024),
        cost_estimate=pl.CostEstimate(flops=flops, bytes_accessed=moved, transcendentals=0),
    )(*args)


def as_sign(values):
    return (2 * values - 1).astype(F32)


def prepare_body(pos, x_ref, a_ref, t_ref, r_ref, cols_ref, rows):
    for k, v in enumerate(
        (x_ref[...].astype(F32), as_sign(a_ref[...]), t_ref[...].astype(F32), as_sign(r_ref[...]))
    ):
        for d in range(G):
            rel = (d - pos[0]) & 3
            for j in range(8):
                at = (8 * d + j) * 128
                rows[rel, k, pl.ds(j, 3, stride=8)] = v[:, at : at + 128]
    cols_ref[...] = rows[...].astype(BF)


def prepare(*args):
    return on_chip_call(
        prepare_body, args, [(G, 4, 24, 128)], scratch=[pltpu.VMEM((G, 4, 24, 128), F32)]
    )[0]


def signs_body(_, s_ref, h_ref, o_ref):
    for k in range(3):
        v = s_ref[k] if k < 2 else h_ref[...]
        o_ref[k * PK : (k + 1) * PK] = pack(as_sign(v)).astype(BF)


def packed_signs(*args):
    return on_chip_call(signs_body, args, [(3 * PK, 128)])[0]


def finish_body(pos, p0, p1, p2, p3, res_ref, inp_ref, rows):
    for j, ref in enumerate((p0, p1, p2, p3)):
        rows[(pos[0] + j) & 3] = ref[...].astype(F32)
    for k, o_ref in enumerate((res_ref, inp_ref)):
        for d in range(G):
            for j in range(8):
                at = (8 * d + j) * 128
                o_ref[:, at : at + 128] = rows[d, pl.ds(24 * k + j, 3, stride=8)].astype(BF)


def finish(*args):
    return on_chip_call(
        finish_body, args, [(3, D), (3, D)], scratch=[pltpu.VMEM((G, 48, 128), F32)]
    )


def perturb_body(s_ref, n_ref, o_ref):
    o_ref[...] = (s_ref[...].astype(F32) * n_ref[...].astype(F32)).astype(BF)


def perturbation(sigmas, noise):
    spec = pl.BlockSpec((1, F, W), lambda i: (i, 0, 0))
    return pl.pallas_call(
        perturb_body,
        grid=(3,),
        in_specs=[spec, spec],
        out_specs=spec,
        out_shape=jax.ShapeDtypeStruct((3, F, W), BF),
        compiler_params=pltpu.CompilerParams(vmem_limit_bytes=8 * 1024 * 1024),
        name="perturbation",
    )(sigmas, noise)


def assemble_body(pos, *refs):
    pieces, (plain_ref, sign_ref, both) = refs[:16], refs[16:]
    zl, y, x, c = pos[1], pos[2], pos[3], pos[4]

    def one_group(g, carry):
        for src in range(2):
            for k in range(2):
                col = c if k == 0 else 1 - c
                for outer in range(4):
                    ref = pieces[8 * src + 4 * k + outer]

                    def place(i, carry):
                        dy, dx = (outer, i) if src == 0 else (i, outer)
                        my = 2 * ((x + dx) & 3) + col
                        for z in range(2):
                            mx = (zl if z == 0 else 1 - zl) * 4 + ((y + dy) & 3)
                            at = pl.ds(pl.multiple_of((mx * 8 + my) * 24, 8), 24)
                            for a in range(2):
                                both[a, at] = ref[i, z, a, g].astype(F32)
                        return carry

                    lax.fori_loop(0, 4, place, 0)
            for a, o_ref in ((0, plain_ref), (1, sign_ref)):
                for j in range(8):
                    o_ref[src, g, :, j * 128 : (j + 1) * 128] = both[a, pl.ds(j, T, stride=8)].astype(BF)
        return carry

    lax.fori_loop(0, G, one_group, 0)


def assemble(pos, pieces):
    return on_chip_call(
        assemble_body, [pos, *pieces], [(2, G, T, W)] * 2, scratch=[pltpu.VMEM((2, ROWS, 128), F32)]
    )


def gather(both, inner, outer):
    line = jnp.stack([both, shift(both, inner, -1), shift(both, inner, 2), shift(both, inner, 1)])
    below = shift(line, outer, 1)
    above = shift(line, outer, -1)
    own = [line, above, shift(below, outer, 1), below]
    return own + [lax.ppermute(p, "c", SWAP) for p in own]


def scale_of(k):
    return jnp.where(k == 2, jnp.float32(SCALE_OUT), jnp.float32(SCALE_IN))


def packed_rows(k):
    return pl.ds(pl.multiple_of(k * PK, 16), PK)


def project_body(rels, pos, x_ref, a_ref, m_ref, p_ref, *refs):
    s_refs, o_ref = refs[:-1], refs[-1]
    for i, rel in enumerate(rels):

        def one(k, carry):
            plain = x_ref[k >> 1, rel]
            flip = plain * a_ref[k >> 1, rel]
            mean = pack(nt(m_ref[k], plain))
            pert = pack(nt(p_ref[k], flip))
            sign = s_refs[i][packed_rows(k)].astype(F32)
            scale = scale_of(k)
            o_ref[i, packed_rows(k)] = (scale * mean + scale * pert * sign).astype(BF)
            return carry

        lax.fori_loop(0, 3, one, 0)


def project(pos, acts, means, perturb, signs, rels):
    return on_chip_call(
        lambda *refs: project_body(rels, *refs),
        [pos, *acts, means, perturb, *(signs[rel] for rel in rels)],
        [(len(rels), 3 * PK, 128)],
        flops=len(rels) * 12 * F * W * T,
    )[0]


def pointwise_body(a_ref, b_ref, c_ref, o_ref):
    def total(k):
        at = slice(k * PK, (k + 1) * PK)
        return a_ref[at].astype(F32) + b_ref[at].astype(F32) + c_ref[at].astype(F32)

    gate, up, dh = total(0), total(1), total(2)
    sig = jax.nn.sigmoid(gate)
    o_ref[0:PK] = (dh * up * sig * (1.0 + gate * (1.0 - sig))).astype(BF)
    o_ref[PK : 2 * PK] = (dh * gate * sig).astype(BF)
    o_ref[2 * PK :] = (gate * sig * up).astype(BF)


def pointwise(pos, a, b, c):
    return on_chip_call(lambda _, *refs: pointwise_body(*refs), [pos, a, b, c], [(3 * PK, 128)])[0]


def back_body(rels, pos, a_ref, m_ref, p_ref, *refs):
    n = len(rels)
    h_refs, s_refs, o_ref, rows = refs[:n], refs[n : 2 * n], refs[2 * n], refs[2 * n + 1]
    c = pos[4]
    for i, rel in enumerate(rels):

        def one(k, carry):
            h = h_refs[i][packed_rows(k)]
            mean = tn(unpack(h), m_ref[k])
            pert = tn(unpack(h * s_refs[i][packed_rows(k)]), p_ref[k])
            scale = scale_of(k)
            v = scale * mean + scale * pert * a_ref[k >> 1, rel].astype(F32)
            for q in range(8):
                at = pl.ds(q, T, stride=8)
                before = jnp.where(k == 1, rows[k >> 1, at], 0.0)
                rows[k >> 1, at] = before + v[:, q * 128 : (q + 1) * 128]
            return carry

        lax.fori_loop(0, 3, one, 0)

        def place(q, carry):
            for j in range(2):
                for col in range(2):
                    at = pl.multiple_of(q * 48 + col * 24, 8)
                    half = c if col == 0 else 1 - c
                    o_ref[half, q, i, j] = rows[1 - j, pl.ds(at, 24)].astype(BF)
            return carry

        lax.fori_loop(0, 32, place, 0)


def back(pos, h, signs, a, means, perturb, rels):
    return on_chip_call(
        lambda *refs: back_body(rels, *refs),
        [pos, a, means, perturb, *h, *(signs[rel] for rel in rels)],
        [(2, 32, len(rels), 2, 24, 128)],
        scratch=[pltpu.VMEM((2, ROWS, 128), F32)],
        flops=len(rels) * 12 * F * W * T,
    )[0]


def grads_body(*refs):
    hs, signs = refs[:4], refs[4:8]
    x_ref, a_ref, n_ref, mo_ref, so_ref, lhs, sums = refs[8:]

    @pl.when(pl.program_id(0) == 0)
    def _():
        def one(k, carry):
            for rel in range(G):
                v = hs[rel][packed_rows(k)]
                lhs[rel, 2 * k] = unpack(v)
                lhs[rel, 2 * k + 1] = unpack(v * signs[rel][packed_rows(k)])
            return carry

        lax.fori_loop(0, 3, one, 0)

    sums[...] = jnp.zeros(sums.shape, F32)

    def one_term(at, carry):
        rel, k = at & 3, at >> 2
        plain = x_ref[k >> 1, rel]
        for j, rhs in enumerate((plain, plain * a_ref[k >> 1, rel])):
            term = scale_of(k) * nn(lhs[rel, 2 * k + j], rhs)
            sums[2 * k + j] += term.astype(BF).astype(F32)
        return carry

    lax.fori_loop(0, 3 * G, one_term, 0)
    for k in range(3):
        mo_ref[k] = sums[2 * k].astype(BF)
        so_ref[k] = (sums[2 * k + 1] * n_ref[k].astype(F32)).astype(BF)


def grads(h, signs, acts, noise):
    w = pl.BlockSpec((3, F, 256), lambda i: (0, 0, i))
    group = pl.BlockSpec((2, G, T, 256), lambda i: (0, 0, 0, i))
    out = jax.ShapeDtypeStruct((3, F, W), BF)
    return pl.pallas_call(
        grads_body,
        grid=(4,),
        in_specs=[ON_CHIP] * 8 + [group] * 2 + [w],
        out_specs=[w, w],
        scratch_shapes=[pltpu.VMEM((G, 6, F, T), BF), pltpu.VMEM((6, F, 256), F32)],
        out_shape=[out, out],
        compiler_params=pltpu.CompilerParams(vmem_limit_bytes=28 * 1024 * 1024),
        cost_estimate=pl.CostEstimate(
            flops=48 * F * W * T, bytes_accessed=8 * G * T * W + 18 * F * W, transcendentals=0
        ),
        name="grads",
    )(*h, *signs, *acts, noise)


def merged(out):
    return (out[0].astype(F32) + lax.ppermute(out[1], "c", SWAP).astype(F32)).astype(BF)


def over_dp(rel):
    return [rel[0]] + [shift(rel[4 - j], "dp", 4 - j) for j in range(1, 4)]


def on_device(
    inputs,
    weight_means,
    weight_sigmas,
    weight_noise,
    input_signs,
    output_signs,
    hidden_signs,
    result_signs,
    cotangent,
):
    place = [lax.axis_index(name) for name in ("dp", "zl", "y", "x", "c")]
    pos = jnp.stack(place).astype(jnp.int32)
    cols = over_dp(prepare(pos, inputs, input_signs, cotangent, result_signs))
    perturb = perturbation(weight_sigmas, weight_noise)
    cols = jnp.stack(cols, axis=1)
    cols = jnp.stack([cols, lax.ppermute(cols, "zl", SWAP)])
    signs = packed_signs(pos, output_signs, hidden_signs)
    below, above = shift(signs, "dp", 1), shift(signs, "dp", -1)
    signs = [signs, above, shift(below, "dp", 1), below]
    xs = gather(cols[:, :2], "x", "y")
    cs = gather(cols[:, 2:], "y", "x")
    acts = assemble(pos, xs + cs)

    half = 3 * PK // 2
    far = project(pos, acts, weight_means, perturb, signs, (2,))[0]
    from_below = shift(far[:half], "dp", 1)
    from_above = shift(far[half:], "dp", -1)
    near = project(pos, acts, weight_means, perturb, signs, (1, 3))

    def plus(u, v):
        return (u.astype(F32) + v.astype(F32)).astype(BF)

    up = jnp.concatenate([plus(near[0, :half], from_below), near[0, half:]])
    down = jnp.concatenate([near[1, :half], plus(near[1, half:], from_above)])
    up, down = shift(up, "dp", 1), shift(down, "dp", -1)
    own = project(pos, acts, weight_means, perturb, signs, (0,))[0]
    h = pointwise(pos, own, up, down)

    below, above, first, second = ring(h, "dp")
    h = [h, above, jnp.concatenate([first, second]), below]
    outs = []
    for rels in ((0,), (1, 3), (2,)):
        outs.append(merged(back(pos, [h[j] for j in rels], signs, acts[1], weight_means, perturb, rels)))
    got = jnp.concatenate(outs, axis=1).reshape(32, 192, 128)
    got = a2a(got, CHIP)
    mean_grad, sigma_grad = grads(h, signs, acts, weight_noise)
    got = jnp.sum(got.astype(F32), axis=0).astype(BF)
    got = over_dp([got[:48], got[48:96], got[144:], got[96:144]])
    result, input_grad = finish(pos, *got)
    return result, input_grad, mean_grad, sigma_grad


def solution(mesh):
    fine = Mesh(mesh.devices.reshape(4, 2, 4, 4, 2), ("dp", "zl", "y", "x", "c"))
    tok = P(("dp", "zl", "y", "x", "c"), None)
    ff = ("zl", "y", "x", "c")
    wide = P(None, ff, "dp")

    return jax.shard_map(
        on_device,
        mesh=fine,
        in_specs=(tok, wide, wide, wide, tok, wide, P(ff, "dp"), tok, tok),
        out_specs=(tok, tok, wide, wide),
        check_vma=False,
    )
```

```python
import jax
import jax.numpy as jnp
from jax import lax
from jax.experimental import pallas as pl
from jax.experimental.pallas import tpu as pltpu
from jax.sharding import Mesh, PartitionSpec as P


D = 4096
FF = 14336
SCALE_IN = D ** (-0.5)
SCALE_OUT = FF ** (-0.5)
F = 224
W = 1024
T = 192
G = 4
PK = 336
CHIP = ("zl", "y", "x")
ROWS = T * 8
SWAP = [(0, 1), (1, 0)]
BF = jnp.bfloat16
F32 = jnp.float32


def a2a(x, axes):
    return lax.all_to_all(x, axes, split_axis=0, concat_axis=0, tiled=True)


def shift(x, axis, by):
    return lax.ppermute(x, axis, [(i, (i + by) % 4) for i in range(4)])


def ring(block, axis):
    half = block.shape[0] // 2
    below, above = shift(block, axis, 1), shift(block, axis, -1)
    return below, above, shift(below[:half], axis, 1), shift(above[half:], axis, -1)


def pack(v):
    rest = jnp.concatenate([v[: F // 2, 128:T], v[F // 2 :, 128:T]], axis=1)
    return jnp.concatenate([v[:, :128], rest], axis=0)


def unpack(v):
    rest = v[F:]
    return jnp.concatenate([v[:F], jnp.concatenate([rest[:, :64], rest[:, 64:]], axis=0)], axis=1)


def nt(a, b):
    return lax.dot_general(a, b, (((1,), (1,)), ((), ())), preferred_element_type=F32)


def tn(a, b):
    return lax.dot_general(a, b, (((0,), (0,)), ((), ())), preferred_element_type=F32)


def nn(a, b):
    return lax.dot_general(a, b, (((1,), (0,)), ((), ())), preferred_element_type=F32)


ON_CHIP = pl.BlockSpec(memory_space=pltpu.VMEM)
SCALARS = pl.BlockSpec(memory_space=pltpu.SMEM)


def on_chip_call(body, args, out, scratch=(), mib=16, flops=0):
    moved = sum(a.size for a in args[1:]) * 2
    return pl.pallas_call(
        body,
        in_specs=[SCALARS] + [ON_CHIP] * (len(args) - 1),
        out_specs=[ON_CHIP] * len(out),
        out_shape=[jax.ShapeDtypeStruct(o, BF) for o in out],
        scratch_shapes=list(scratch),
        compiler_params=pltpu.CompilerParams(vmem_limit_bytes=mib * 1024 * 1024),
        cost_estimate=pl.CostEstimate(flops=flops, bytes_accessed=moved, transcendentals=0),
    )(*args)


def as_sign(values):
    return (2 * values - 1).astype(F32)


def prepare_body(pos, x_ref, a_ref, t_ref, r_ref, cols_ref, rows):
    for k, v in enumerate(
        (x_ref[...].astype(F32), as_sign(a_ref[...]), t_ref[...].astype(F32), as_sign(r_ref[...]))
    ):
        for d in range(G):
            rel = (d - pos[0]) & 3
            for j in range(8):
                at = (8 * d + j) * 128
                rows[rel, k, pl.ds(j, 3, stride=8)] = v[:, at : at + 128]
    cols_ref[...] = rows[...].astype(BF)


def prepare(*args):
    return on_chip_call(
        prepare_body, args, [(G, 4, 24, 128)], scratch=[pltpu.VMEM((G, 4, 24, 128), F32)]
    )[0]


def signs_body(_, s_ref, h_ref, o_ref):
    for k in range(3):
        v = s_ref[k] if k < 2 else h_ref[...]
        o_ref[k * PK : (k + 1) * PK] = pack(as_sign(v)).astype(BF)


def packed_signs(*args):
    return on_chip_call(signs_body, args, [(3 * PK, 128)])[0]


def finish_body(pos, p0, p1, p2, p3, res_ref, inp_ref, rows):
    for j, ref in enumerate((p0, p1, p2, p3)):
        rows[(pos[0] + j) & 3] = ref[...].astype(F32)
    for k, o_ref in enumerate((res_ref, inp_ref)):
        for d in range(G):
            for j in range(8):
                at = (8 * d + j) * 128
                o_ref[:, at : at + 128] = rows[d, pl.ds(24 * k + j, 3, stride=8)].astype(BF)


def finish(*args):
    return on_chip_call(
        finish_body, args, [(3, D), (3, D)], scratch=[pltpu.VMEM((G, 48, 128), F32)]
    )


def perturb_body(s_ref, n_ref, o_ref):
    o_ref[...] = (s_ref[...].astype(F32) * n_ref[...].astype(F32)).astype(BF)


def perturbation(sigmas, noise):
    spec = pl.BlockSpec((1, F, W), lambda i: (i, 0, 0))
    return pl.pallas_call(
        perturb_body,
        grid=(3,),
        in_specs=[spec, spec],
        out_specs=spec,
        out_shape=jax.ShapeDtypeStruct((3, F, W), BF),
        compiler_params=pltpu.CompilerParams(vmem_limit_bytes=8 * 1024 * 1024),
        name="perturbation",
    )(sigmas, noise)


def assemble_body(pos, *refs):
    pieces, (plain_ref, sign_ref, both) = refs[:16], refs[16:]
    zl, y, x, c = pos[1], pos[2], pos[3], pos[4]

    def one_group(g, carry):
        for src in range(2):
            for k in range(2):
                col = c if k == 0 else 1 - c
                for outer in range(4):
                    ref = pieces[8 * src + 4 * k + outer]

                    def place(i, carry):
                        dy, dx = (outer, i) if src == 0 else (i, outer)
                        my = 2 * ((x + dx) & 3) + col
                        for z in range(2):
                            mx = (zl if z == 0 else 1 - zl) * 4 + ((y + dy) & 3)
                            at = pl.ds(pl.multiple_of((mx * 8 + my) * 24, 8), 24)
                            for a in range(2):
                                both[a, at] = ref[i, z, a, g].astype(F32)
                        return carry

                    lax.fori_loop(0, 4, place, 0, unroll=True)
            for a, o_ref in ((0, plain_ref), (1, sign_ref)):
                for j in range(8):
                    o_ref[src, g, :, j * 128 : (j + 1) * 128] = both[a, pl.ds(j, T, stride=8)].astype(BF)
        return carry

    lax.fori_loop(0, G, one_group, 0)


def assemble(pos, pieces):
    return on_chip_call(
        assemble_body, [pos, *pieces], [(2, G, T, W)] * 2, scratch=[pltpu.VMEM((2, ROWS, 128), F32)]
    )


def gather(both, inner, outer):
    line = jnp.stack([both, shift(both, inner, -1), shift(both, inner, 2), shift(both, inner, 1)])
    below = shift(line, outer, 1)
    above = shift(line, outer, -1)
    own = [line, above, shift(below, outer, 1), below]
    return own + [lax.ppermute(p, "c", SWAP) for p in own]


def scale_of(k):
    return jnp.where(k == 2, jnp.float32(SCALE_OUT), jnp.float32(SCALE_IN))


def packed_rows(k):
    return pl.ds(pl.multiple_of(k * PK, 16), PK)


def split_step(step, rels):
    i = jnp.where(step >= 3, 1, 0)
    return i, rels[0] + i * (rels[-1] - rels[0]), step - 3 * i


def project_body(rels, pos, x_ref, a_ref, m_ref, p_ref, *refs):
    n = len(rels)
    s_refs, o_ref, signs = refs[:n], refs[n], refs[n + 1]
    for i in range(n):
        signs[i] = s_refs[i][...]

    def one(step, carry):
        i, rel, k = split_step(step, rels)
        plain = x_ref[k >> 1, rel]
        flip = plain * a_ref[k >> 1, rel]
        mean = pack(nt(m_ref[k], plain))
        pert = pack(nt(p_ref[k], flip))
        sign = signs[i, packed_rows(k)].astype(F32)
        scale = scale_of(k)
        o_ref[i, packed_rows(k)] = (scale * mean + scale * pert * sign).astype(BF)
        return carry

    lax.fori_loop(0, 3 * n, one, 0)


def project(pos, acts, means, perturb, signs, rels):
    return on_chip_call(
        lambda *refs: project_body(rels, *refs),
        [pos, *acts, means, perturb, *(signs[rel] for rel in rels)],
        [(len(rels), 3 * PK, 128)],
        scratch=[pltpu.VMEM((len(rels), 3 * PK, 128), BF)],
        flops=len(rels) * 12 * F * W * T,
    )[0]


def pointwise_body(a_ref, b_ref, c_ref, o_ref):
    def total(k):
        at = slice(k * PK, (k + 1) * PK)
        return a_ref[at].astype(F32) + b_ref[at].astype(F32) + c_ref[at].astype(F32)

    gate, up, dh = total(0), total(1), total(2)
    sig = jax.nn.sigmoid(gate)
    o_ref[0:PK] = (dh * up * sig * (1.0 + gate * (1.0 - sig))).astype(BF)
    o_ref[PK : 2 * PK] = (dh * gate * sig).astype(BF)
    o_ref[2 * PK :] = (gate * sig * up).astype(BF)


def pointwise(pos, a, b, c):
    return on_chip_call(lambda _, *refs: pointwise_body(*refs), [pos, a, b, c], [(3 * PK, 128)])[0]


def back_body(rels, pos, a_ref, m_ref, p_ref, *refs):
    n = len(rels)
    o_ref, rows, acts, signs = refs[2 * n :]
    c = pos[4]
    for i in range(n):
        acts[i], signs[i] = refs[i][...], refs[n + i][...]

    def one(step, carry):
        i, rel, k = split_step(step, rels)
        h = acts[i, packed_rows(k)]
        mean = tn(unpack(h), m_ref[k])
        pert = tn(unpack(h * signs[i, packed_rows(k)]), p_ref[k])
        scale = scale_of(k)
        v = scale * mean + scale * pert * a_ref[k >> 1, rel].astype(F32)
        for q in range(8):
            at = pl.ds(q, T, stride=8)
            before = jnp.where(k == 1, rows[i, k >> 1, at], 0.0)
            rows[i, k >> 1, at] = before + v[:, q * 128 : (q + 1) * 128]
        return carry

    lax.fori_loop(0, 3 * n, one, 0)

    def place(q, carry):
        for i in range(n):
            for j in range(2):
                for col in range(2):
                    at = pl.multiple_of(q * 48 + col * 24, 8)
                    half = c if col == 0 else 1 - c
                    o_ref[half, q, i, j] = rows[i, 1 - j, pl.ds(at, 24)].astype(BF)
        return carry

    lax.fori_loop(0, 32, place, 0, unroll=2)


def back(pos, h, signs, a, means, perturb, rels):
    return on_chip_call(
        lambda *refs: back_body(rels, *refs),
        [pos, a, means, perturb, *h, *(signs[rel] for rel in rels)],
        [(2, 32, len(rels), 2, 24, 128)],
        scratch=[pltpu.VMEM((len(rels), 2, ROWS, 128), F32)]
        + [pltpu.VMEM((len(rels), 3 * PK, 128), BF)] * 2,
        flops=len(rels) * 12 * F * W * T,
    )[0]


def grads_body(*refs):
    hs, signs = refs[:4], refs[4:8]
    x_ref, a_ref, n_ref, mo_ref, so_ref, lhs, sums = refs[8:]

    @pl.when(pl.program_id(0) == 0)
    def _():
        def one(k, carry):
            for rel in range(G):
                v = hs[rel][packed_rows(k)]
                lhs[rel, 2 * k] = unpack(v)
                lhs[rel, 2 * k + 1] = unpack(v * signs[rel][packed_rows(k)])
            return carry

        lax.fori_loop(0, 3, one, 0)

    sums[...] = jnp.zeros(sums.shape, F32)

    def one_term(at, carry):
        rel, k = at & 3, at >> 2
        plain = x_ref[k >> 1, rel]
        for j, rhs in enumerate((plain, plain * a_ref[k >> 1, rel])):
            term = scale_of(k) * nn(lhs[rel, 2 * k + j], rhs)
            sums[2 * k + j] += term.astype(BF).astype(F32)
        return carry

    lax.fori_loop(0, 3 * G, one_term, 0)
    for k in range(3):
        mo_ref[k] = sums[2 * k].astype(BF)
        so_ref[k] = (sums[2 * k + 1] * n_ref[k].astype(F32)).astype(BF)


def grads(h, signs, acts, noise):
    w = pl.BlockSpec((3, F, 512), lambda i: (0, 0, i))
    group = pl.BlockSpec((2, G, T, 512), lambda i: (0, 0, 0, i))
    packed = pl.BlockSpec((3 * PK, 128), lambda i: (0, 0))
    out = jax.ShapeDtypeStruct((3, F, W), BF)
    return pl.pallas_call(
        grads_body,
        grid=(2,),
        in_specs=[packed] * 8 + [group] * 2 + [w],
        out_specs=[w, w],
        scratch_shapes=[pltpu.VMEM((G, 6, F, T), BF), pltpu.VMEM((6, F, 512), F32)],
        out_shape=[out, out],
        compiler_params=pltpu.CompilerParams(vmem_limit_bytes=28 * 1024 * 1024),
        cost_estimate=pl.CostEstimate(
            flops=48 * F * W * T, bytes_accessed=8 * G * T * W + 18 * F * W, transcendentals=0
        ),
        name="grads",
    )(*h, *signs, *acts, noise)


def merged(out):
    return (out[0].astype(F32) + lax.ppermute(out[1], "c", SWAP).astype(F32)).astype(BF)


def over_dp(rel):
    return [rel[0]] + [shift(rel[4 - j], "dp", 4 - j) for j in range(1, 4)]


def on_device(
    inputs,
    weight_means,
    weight_sigmas,
    weight_noise,
    input_signs,
    output_signs,
    hidden_signs,
    result_signs,
    cotangent,
):
    place = [lax.axis_index(name) for name in ("dp", "zl", "y", "x", "c")]
    pos = jnp.stack(place).astype(jnp.int32)
    cols = over_dp(prepare(pos, inputs, input_signs, cotangent, result_signs))
    perturb = perturbation(weight_sigmas, weight_noise)
    cols = jnp.stack(cols, axis=1)
    cols = jnp.stack([cols, lax.ppermute(cols, "zl", SWAP)])
    signs = packed_signs(pos, output_signs, hidden_signs)
    below, above = shift(signs, "dp", 1), shift(signs, "dp", -1)
    signs = [signs, above, shift(below, "dp", 1), below]
    xs = gather(cols[:, :2], "x", "y")
    cs = gather(cols[:, 2:], "y", "x")
    acts = assemble(pos, xs + cs)

    half = 3 * PK // 2
    far = project(pos, acts, weight_means, perturb, signs, (2,))[0]
    from_below = shift(far[:half], "dp", 1)
    from_above = shift(far[half:], "dp", -1)
    near = project(pos, acts, weight_means, perturb, signs, (1, 3))

    def plus(u, v):
        return (u.astype(F32) + v.astype(F32)).astype(BF)

    up = jnp.concatenate([plus(near[0, :half], from_below), near[0, half:]])
    down = jnp.concatenate([near[1, :half], plus(near[1, half:], from_above)])
    up, down = shift(up, "dp", 1), shift(down, "dp", -1)
    own = project(pos, acts, weight_means, perturb, signs, (0,))[0]
    h = pointwise(pos, own, up, down)

    below, above, first, second = ring(h, "dp")
    h = [h, above, jnp.concatenate([first, second]), below]
    outs = []
    for rels in ((0,), (1, 3), (2,)):
        outs.append(merged(back(pos, [h[j] for j in rels], signs, acts[1], weight_means, perturb, rels)))
    got = jnp.concatenate(outs, axis=1).reshape(32, 192, 128)
    got = a2a(got, CHIP)
    mean_grad, sigma_grad = grads(h, signs, acts, weight_noise)
    got = jnp.sum(got.astype(F32), axis=0).astype(BF)
    got = over_dp([got[:48], got[48:96], got[144:], got[96:144]])
    result, input_grad = finish(pos, *got)
    return result, input_grad, mean_grad, sigma_grad


def solution(mesh):
    fine = Mesh(mesh.devices.reshape(4, 2, 4, 4, 2), ("dp", "zl", "y", "x", "c"))
    tok = P(("dp", "zl", "y", "x", "c"), None)
    ff = ("zl", "y", "x", "c")
    wide = P(None, ff, "dp")

    return jax.shard_map(
        on_device,
        mesh=fine,
        in_specs=(tok, wide, wide, wide, tok, wide, P(ff, "dp"), tok, tok),
        out_specs=(tok, tok, wide, wide),
        check_vma=False,
    )
```
